128 devices in a mesh: user: 4 (over x_hi, core), tok: 32 (over z, y, x_lo).
Axes of the slice: x: 4 (x_hi: 2, x_lo: 2; x = x_hi * 2 + x_lo), y: 4, z: 4, core: 2. Of those that a mesh axis runs over, the one named last changes fastest.
Arguments:
- hidden: bfloat16 [4, 4096, 16384], P('user', 'tok'), may hold values from -256 to 256, as said below
- cotangent: bfloat16 [4, 4096, 2048], P('user', 'tok'), may hold values from -6 to 6
- lengths: int32 [4], P('user'), may hold values from 1024 to 4096
Outputs:
- clipped_sum: float32 [16384, 2048], P('tok', 'user')
The draws below stay inside these ranges and needn't reach their ends.
Inputs may be any that keep to these rules, and one draw needn't show every extreme that they name: bfloat16 activations of mixed magnitudes across tokens and hidden units.
All inputs are finite; a program needn't handle non-finite values.
Results may differ from the reference program's by a relative error of at most 0.0003.
Values may be sent and summed in bfloat16 or wider, within the bound.
A program may use at most 128 MiB of HBM per device.

```python
import math
import jax
import jax.numpy as jnp
from jax import lax

D = 2048
FF = 16384
CAP = 4096
USERS = 4


def draw_hidden(key, part):
    key_base = jax.random.fold_in(key, 11)
    key_cols = jax.random.fold_in(key, 12)
    key_rows = jax.random.fold_in(key, 13)
    base = jnp.clip(jax.random.normal(key_base, (USERS, CAP, FF), jnp.float32), -6.0, 6.0)
    trend = jnp.exp(math.log(3.0) * jnp.arange(FF, dtype=jnp.float32) / FF)
    column = jnp.exp(jax.random.uniform(key_cols, (FF,), jnp.float32, -1.15, 1.15)) * trend
    row_scale = jnp.exp(jax.random.uniform(key_rows, (USERS, CAP, 1), jnp.float32, math.log(0.3), math.log(3.0)))
    values = base * row_scale * column
    return jnp.clip(values, -256.0, 256.0).astype(jnp.bfloat16)


def with_ends(entries, rng, smallest, largest):
    index_at = [jax.random.randint(jax.random.fold_in(rng, axis), (), 0, length) for axis, length in enumerate(entries.shape)]
    longest = entries.shape.index(max(entries.shape))
    neighbour = index_at[:longest] + [(index_at[longest] + 1) % entries.shape[longest]] + index_at[longest + 1:]
    return entries.at[tuple(index_at)].set(smallest).at[tuple(neighbour)].set(largest)


def levels(stream_key, extent, split, least, largest):
    level, own = 1.0, jax.random.fold_in(stream_key, 6)
    for axis_at, blocks in split:
        steps = jnp.exp(jax.random.uniform(jax.random.fold_in(own, axis_at), (blocks,), jnp.float32, least / len(split), largest / len(split)))
        level = level * jnp.repeat(steps, extent[axis_at] // blocks).reshape([-1 if axis == axis_at else 1 for axis in range(len(extent))])
    return level


def normal_values(own_key, shape, scale, reach, pieces=(), kind=jnp.bfloat16):
    array = scale * jax.random.normal(own_key, shape, jnp.float32)
    if pieces:
        array = array * levels(own_key, shape, pieces, -0.22, 0.18)
    return jnp.clip(array, -reach, reach).astype(kind)


def setup_inputs(seed: int = 0) -> dict:
    seeds = jax.random.split(jax.random.key(seed), 4)
    return {
        "hidden": draw_hidden(jax.random.fold_in(seeds[3], 71), 0),
        "cotangent": normal_values(seeds[1], (USERS, CAP, D), 1.0, 6.0, ((0, 4), (1, 32))),
        "lengths": with_ends(jax.random.randint(seeds[2], (USERS,), CAP // 4, CAP + 1), jax.random.fold_in(seeds[2], 1), CAP // 4, CAP).astype(jnp.int32),
    }


epsilon = 1e-06

def reference(hidden, cotangent, lengths):
    clip_bound = math.sqrt(8.0 * FF * D * CAP)
    scaling = math.sqrt(FF * D) / (USERS * clip_bound)

    def one_user(running, inputs):
        user_rows, user_cot, user_length = inputs
        keep_rows = jnp.arange(CAP, dtype=jnp.int32) < user_length
        masked = jnp.where(keep_rows[:, None], user_cot, jnp.zeros_like(user_cot))
        gradient = jnp.dot(user_rows.astype(jnp.float32).T, masked.astype(jnp.float32), precision=lax.Precision.HIGHEST)
        norm_sq = jnp.sum(gradient * gradient)
        factor = jnp.minimum(1.0, clip_bound / jnp.sqrt(norm_sq + epsilon)) * scaling
        return (running + factor * gradient, None)
    running, unused = lax.scan(one_user, jnp.zeros((FF, D), jnp.float32), (hidden, cotangent, lengths))
    return running
```

```python
import functools
import math

import jax
import jax.numpy as jnp
from jax import lax
from jax.experimental import pallas as pl
from jax.experimental.pallas import tpu as pltpu
from jax.sharding import PartitionSpec as P

epsilon = 1e-06
MESH = pl.DeviceIdType.MESH
LEVELS = 32767.0


def device(xh, xl, y, z, core):
    return (xh * 2 + core, (z * 4 + y) * 2 + xl)


def remote(src, dst, send, recv, where):
    return pltpu.make_async_remote_copy(
        src_ref=src, dst_ref=dst, send_sem=send, recv_sem=recv, device_id=where, device_id_type=MESH
    )


def take(ref, sem):
    pltpu.make_async_copy(ref, ref, sem).wait()


def coded(block):
    peak = jnp.max(jnp.abs(block), axis=0, keepdims=True)
    ok = peak > 1e-30
    step = jnp.where(ok, peak * (1.0 / LEVELS), 0.0)
    inverse = jnp.where(ok, LEVELS / jnp.where(ok, peak, 1.0), 0.0)
    code = jnp.round(block * inverse).astype(jnp.int32).astype(jnp.int16)
    return code, step


def kernel(
    clip_bound, scaling,
    lengths, hidden, cotangent, out,
    masked, cols, rows, turned, t_code, t_step, t_got, t_gotstep,
    x_code, x_step, x_got, x_gotstep, square, near, far,
    swap_s, swap_r, ring_s, ring_r, side_s, side_r, rows_s, rows_r,
    ts_s, ts_r, tt_s, tt_r, xs_s, xs_r, xt_s, xt_r, near_s, near_r, far_s, far_r,
):
    user, tok = lax.axis_index("user"), lax.axis_index("tok")
    xh, core = user // 2, user % 2
    xl, y, z = tok % 2, (tok // 2) % 4, tok // 8
    zi = z % 2
    zmate = z + 1 - 2 * zi
    ztwin = 3 - z
    home = xl == core
    up, down, across = (y + 1) % 4, (y + 3) % 4, (y + 2) % 4
    shard = zi * 4 + y

    def send_rows(kind, k):
        slot = kind * 2 + k
        for dy, dz, cc in [(1, 0, 0), (3, 1, 1), (2, 0, 1), (0, 1, 0), (3, 0, 0), (1, 1, 1), (0, 1, 1), (2, 1, 0),
                           (1, 0, 1), (3, 1, 0), (2, 0, 0), (3, 0, 1), (2, 1, 1), (1, 1, 0), (0, 0, 0), (0, 0, 1)]:
            y2 = (y + dy) % 4
            z2 = zmate if dz else z
            zrow = z2 if kind else 3 - z2
            start = ((zrow * 4 + y2) * 2 + cc) * 512 + k * 256
            src = hidden.at[0, :, pl.ds(pl.multiple_of(start, 256), 256)]
            dst = rows.at[slot, shard * 2 + xl]
            where = device(xh, core, y2, z2, cc)
            if dy == 0 and dz == 0:
                mine = jnp.logical_and(home, core == cc)

                @pl.when(mine)
                def _():
                    pltpu.make_async_copy(src, dst, rows_r.at[slot]).start()

                @pl.when(jnp.logical_not(mine))
                def _():
                    remote(src, dst, rows_s.at[slot], rows_r.at[slot], where).start()
            else:
                remote(src, dst, rows_s.at[slot], rows_r.at[slot], where).start()

    token = tok * 128 + lax.broadcasted_iota(jnp.int32, (128, 256), 0)
    keep = token < lengths[0]
    for p in range(8):
        masked[p] = jnp.where(keep, cotangent[0, :, p * 256:(p + 1) * 256], jnp.zeros((128, 256), jnp.bfloat16))

    spot = pl.ds(pl.multiple_of(xl * 128, 128), 128)

    def swap(lane):
        src = masked.at[lane * 4:lane * 4 + 4]
        dst = cols.at[lane * 4:lane * 4 + 4, shard, spot]
        return src, dst

    for lane in (0, 1):
        src, dst = swap(lane)
        mine = jnp.logical_and(home, core == lane)

        @pl.when(mine)
        def _():
            pltpu.make_async_copy(src, dst, swap_r.at[xl]).start()

        @pl.when(jnp.logical_not(mine))
        def _():
            remote(src, dst, swap_s.at[lane], swap_r.at[xl], device(xh, core, y, z, lane)).start()

    send_rows(0, 0)

    for half in (0, 1):
        take(masked.at[0:4], swap_r.at[half])

    def piece(p, which, part=None):
        ref = cols.at[p, which]
        if part is None:
            return ref
        return ref.at[part * 128:part * 128 + 128]

    def pass_on(p, which, sem, where, part=None):
        ref = piece(p, which, part)
        remote(ref, ref, ring_s, ring_r.at[sem], where).start()

    def got(p, sem, part=None):
        take(piece(p, 0, part), ring_r.at[sem])

    @pl.when(core == 0)
    def _():
        here = lambda y2, z2: device(xh, xl, y2, z2, 0)
        for p in range(4):
            pass_on(p, shard, p, here(y, zmate))
            pass_on(p, shard, 4 + p, here(up, z))
            pass_on(p, shard, 12 + p, here(down, z))
        send_rows(0, 1)
        mate = (1 - zi) * 4
        for p in range(4):
            got(p, p)
            pass_on(p, mate + y, 8 + p, here(up, z))
            pass_on(p, mate + y, 16 + p, here(down, z))
        for m in (0, 1):
            base = mate if m else zi * 4
            for p in range(4):
                got(p, 4 + m * 4 + p)
                pass_on(p, base + down, 20 + m * 4 + p, here(up, z), 0)
                got(p, 12 + m * 4 + p)
                pass_on(p, base + up, 28 + m * 4 + p, here(down, z), 1)
        for p in range(4):
            for m in (0, 1):
                got(p, 20 + m * 4 + p, 0)
                got(p, 28 + m * 4 + p, 1)
            remote(cols.at[p], cols.at[p], side_s.at[p], side_r.at[p], device(xh, xl, y, z, 1)).start()

    @pl.when(core == 1)
    def _():
        here = lambda y2, z2: device(xh, xl, y2, z2, 1)
        own = zi * 4
        for p in range(4):
            pass_on(4 + p, shard, p, here(up, z))
            pass_on(4 + p, shard, 4 + p, here(down, z))
            pass_on(4 + p, shard, 16 + p, here(y, zmate))
        send_rows(0, 1)
        for p in range(4):
            got(4 + p, p)
            pass_on(4 + p, own + down, 8 + p, here(up, z), 0)
            pass_on(4 + p, own + down, 20 + p, here(y, zmate))
            got(4 + p, 4 + p)
            pass_on(4 + p, own + up, 12 + p, here(down, z), 1)
            pass_on(4 + p, own + up, 24 + p, here(y, zmate))
        for p in range(4):
            got(4 + p, 8 + p, 0)
            got(4 + p, 12 + p, 1)
            pass_on(4 + p, own + across, 28 + p, here(y, zmate))
        for p in range(4):
            for kind in range(4):
                got(4 + p, 16 + kind * 4 + p)
            remote(cols.at[4 + p], cols.at[4 + p], side_s.at[p], side_r.at[p], device(xh, xl, y, z, 0)).start()

    send_rows(1, 0)
    for p in range(4):
        take(cols.at[0], side_r.at[p])
    send_rows(1, 1)

    def turn(slot):
        take(rows.at[slot], rows_r.at[slot])
        for s in range(16):
            turned[:, s * 128:(s + 1) * 128] = rows[slot, s].T

    def product(piece_at):
        right = cols[piece_at].reshape(2048, 256)
        return lax.dot_general(turned[...], right, (((1,), (0,)), ((), ())), preferred_element_type=jnp.float32)

    def target(jj):
        return jnp.where(jj < 2, 1 - xh, xh), jj % 2

    twin = device(xh, xl, y, ztwin, core)

    def t_data(k, jj):
        return remote(t_code.at[k, jj], t_got.at[k, jj], ts_s.at[k, jj], ts_r.at[k, jj], twin)

    def t_scale(k, jj):
        return remote(t_step.at[k, jj], t_gotstep.at[k, jj], tt_s.at[k, jj], tt_r.at[k, jj], twin)

    def t_pass(k, carry):
        turn(k)

        def one(jj, inner):
            xt, jc = target(jj)
            for h in (0, 1):
                code, step = coded(product((xt * 2 + jc) * 2 + h))
                t_code[k, jj, h] = code
                t_step[k, jj, h] = jnp.broadcast_to(step, (8, 256))
            t_data(k, jj).start()
            t_scale(k, jj).start()
            return inner

        return lax.fori_loop(0, 4, one, carry)

    lax.fori_loop(0, 2, t_pass, 0)

    square[...] = jnp.zeros_like(square)
    slot_x = xh * 2 + xl

    def x_parts(k, jj):
        xt, jc = target(jj)
        mine = jnp.logical_and(jnp.logical_and(xt == xh, home), jc == core)
        where = device(xt, core, y, z, jc)
        data = (x_code.at[k, jj], x_got.at[slot_x, k])
        scale = (x_step.at[k, jj], x_gotstep.at[slot_x, k])
        return mine, where, data, scale

    def o_pass(k, carry):
        turn(2 + k)

        def one(jj, inner):
            xt, jc = target(jj)
            take(t_got.at[k, jj], ts_r.at[k, jj])
            take(t_gotstep.at[k, jj], tt_r.at[k, jj])
            for h in (0, 1):
                value = product((xt * 2 + jc) * 2 + h)
                value = value + t_got[k, jj, h].astype(jnp.int32).astype(jnp.float32) * t_gotstep[k, jj, h, 0:1]
                square[...] += jnp.sum((value * value).reshape(32, 8, 256), axis=0)
                code, step = coded(value)
                x_code[k, jj, h] = code
                x_step[k, jj, h] = jnp.broadcast_to(step, (8, 256))
            mine, where, data, scale = x_parts(k, jj)

            @pl.when(mine)
            def _():
                pltpu.make_async_copy(*data, xs_r.at[slot_x, k]).start()
                pltpu.make_async_copy(*scale, xt_r.at[slot_x, k]).start()

            @pl.when(jnp.logical_not(mine))
            def _():
                remote(*data, xs_s.at[k, jj], xs_r.at[slot_x, k], where).start()
                remote(*scale, xt_s.at[k, jj], xt_r.at[slot_x, k], where).start()

            return inner

        return lax.fori_loop(0, 4, one, carry)

    lax.fori_loop(0, 2, o_pass, 0)

    spot1 = z * 2 + core
    near[spot1] = square[:, 0:128] + square[:, 128:256]
    for dz in range(4):
        for dc in range(2):
            if (dz, dc) != (0, 0):
                remote(near.at[spot1], near.at[spot1], near_s, near_r,
                       device(xh, xl, y, (z + dz) % 4, (core + dc) % 2)).start()
    take(near.at[0:7], near_r)
    spot2 = slot_x * 4 + y
    far[spot2] = jnp.sum(near[...], axis=0)
    for dh in range(2):
        for dl in range(2):
            for dy in range(4):
                if (dh, dl, dy) != (0, 0, 0):
                    remote(far.at[spot2], far.at[spot2], far_s, far_r,
                           device((xh + dh) % 2, (xl + dl) % 2, (y + dy) % 4, z, core)).start()
    take(far.at[0:15], far_r)

    factors = []
    for x in range(4):
        total = jnp.sum(far[x * 4] + far[x * 4 + 1] + far[x * 4 + 2] + far[x * 4 + 3], axis=(0, 1), keepdims=True)
        factors.append(jnp.minimum(1.0, clip_bound / jnp.sqrt(total + epsilon)) * scaling)

    for k in range(2):
        for x in range(4):
            take(x_got.at[x, k], xs_r.at[x, k])
            take(x_gotstep.at[x, k], xt_r.at[x, k])
        for h in (0, 1):
            total = None
            for x in range(4):
                weight = factors[x] * x_gotstep[x, k, h, 0:1]
                term = x_got[x, k, h].astype(jnp.int32).astype(jnp.float32) * weight
                total = term if total is None else total + term
            out[k * 256:(k + 1) * 256, h * 256:(h + 1) * 256] = total

    for lane in (0, 1):
        src, dst = swap(lane)

        @pl.when(jnp.logical_not(jnp.logical_and(home, core == lane)))
        def _():
            take(src, swap_s.at[lane])

    take(cols.at[0:7, 0:4], ring_s)
    for p in range(4):
        take(cols.at[0], side_s.at[p])
    for slot in range(4):
        @pl.when(home)
        def _():
            take(rows.at[slot, 0:15], rows_s.at[slot])

        @pl.when(jnp.logical_not(home))
        def _():
            take(rows.at[slot], rows_s.at[slot])
    for k in range(2):
        for jj in range(4):
            take(t_code.at[k, jj], ts_s.at[k, jj])
            take(t_step.at[k, jj], tt_s.at[k, jj])
            mine = x_parts(k, jj)[0]

            @pl.when(jnp.logical_not(mine))
            def _():
                take(x_code.at[k, jj], xs_s.at[k, jj])
                take(x_step.at[k, jj], xt_s.at[k, jj])
    take(near.at[0:7], near_s)
    take(far.at[0:15], far_s)


def body(hidden, cotangent, lengths):
    tok_count = lax.axis_size("tok")
    user_count = lax.axis_size("user")
    hidden_width = hidden.shape[2]
    model_width = cotangent.shape[2]
    capacity = hidden.shape[1] * tok_count
    clip_bound = math.sqrt(8.0 * hidden_width * model_width * capacity)
    scaling = math.sqrt(hidden_width * model_width) / (user_count * clip_bound)
    half, full, word = jnp.bfloat16, jnp.float32, jnp.int16
    dma = pltpu.SemaphoreType.DMA
    return pl.pallas_call(
        functools.partial(kernel, clip_bound, scaling),
        out_shape=jax.ShapeDtypeStruct((512, 512), full),
        in_specs=[
            pl.BlockSpec(memory_space=pltpu.SMEM),
            pl.BlockSpec(memory_space=pl.ANY),
            pl.BlockSpec(memory_space=pltpu.VMEM),
        ],
        out_specs=pl.BlockSpec(memory_space=pltpu.VMEM),
        scratch_shapes=[
            pltpu.VMEM((8, 128, 256), half),
            pltpu.VMEM((8, 8, 256, 256), half),
            pltpu.VMEM((4, 16, 128, 256), half),
            pltpu.VMEM((256, 2048), half),
            pltpu.VMEM((2, 4, 2, 256, 256), word),
            pltpu.VMEM((2, 4, 2, 8, 256), full),
            pltpu.VMEM((2, 4, 2, 256, 256), word),
            pltpu.VMEM((2, 4, 2, 8, 256), full),
            pltpu.VMEM((2, 4, 2, 256, 256), word),
            pltpu.VMEM((2, 4, 2, 8, 256), full),
            pltpu.VMEM((4, 2, 2, 256, 256), word),
            pltpu.VMEM((4, 2, 2, 8, 256), full),
            pltpu.VMEM((8, 256), full),
            pltpu.VMEM((8, 8, 128), full),
            pltpu.VMEM((16, 8, 128), full),
            dma((2,)), dma((2,)), dma, dma((36,)), dma((4,)), dma((4,)), dma((4,)), dma((4,)),
            dma((2, 4)), dma((2, 4)), dma((2, 4)), dma((2, 4)),
            dma((2, 4)), dma((4, 2)), dma((2, 4)), dma((4, 2)),
            dma, dma, dma, dma,
        ],
        compiler_params=pltpu.CompilerParams(has_side_effects=True, vmem_limit_bytes=56 << 20),
        name="clipped_sum",
    )(lengths, hidden, cotangent)


def solution(mesh):
    return jax.shard_map(
        body,
        mesh=mesh,
        in_specs=(P("user", "tok", None), P("user", "tok", None), P("user")),
        out_specs=P("tok", "user"),
        check_vma=False,
    )
```

```python
import functools
import math

import jax
import jax.numpy as jnp
from jax import lax
from jax.experimental import pallas as pl
from jax.experimental.pallas import tpu as pltpu
from jax.sharding import PartitionSpec as P

epsilon = 1e-06
MESH = pl.DeviceIdType.MESH
LEVELS = 32767.0
ORDER = [(1, 0, 0), (3, 1, 1), (2, 0, 1), (0, 1, 0), (3, 0, 0), (1, 1, 1), (0, 1, 1), (2, 1, 0),
         (1, 0, 1), (3, 1, 0), (2, 0, 0), (3, 0, 1), (2, 1, 1), (1, 1, 0), (0, 0, 0), (0, 0, 1)]
PACE = (16, 0, 0, 0, 0, 0, 0, 16, 16, 16, 0, 0, 0)


def device(xh, xl, y, z, core):
    return (xh * 2 + core, (z * 4 + y) * 2 + xl)


def remote(src, dst, send, recv, where):
    return pltpu.make_async_remote_copy(
        src_ref=src, dst_ref=dst, send_sem=send, recv_sem=recv, device_id=where, device_id_type=MESH
    )


def take(ref, sem):
    pltpu.make_async_copy(ref, ref, sem).wait()


def coded(block):
    peak = jnp.max(jnp.abs(block), axis=0, keepdims=True)
    ok = peak > 1e-30
    step = jnp.where(ok, peak * (1.0 / LEVELS), 0.0)
    inverse = jnp.where(ok, LEVELS / jnp.where(ok, peak, 1.0), 0.0)
    code = jnp.round(block * inverse).astype(jnp.int32).astype(jnp.int16)
    return code, step


def kernel(
    clip_bound, scaling,
    lengths, hidden, cotangent, out,
    masked, cols, rows, turned, t_code, t_step, t_got, t_gotstep,
    x_code, x_step, x_got, x_gotstep, square, near, far,
    swap_s, swap_r, ring_s, ring_r, side_s, side_r, rows_s, rows_r,
    ts_s, ts_r, tt_s, tt_r, xs_s, xs_r, xt_s, xt_r, near_s, near_r, far_s, far_r,
):
    user, tok = lax.axis_index("user"), lax.axis_index("tok")
    xh, core = user // 2, user % 2
    xl, y, z = tok % 2, (tok // 2) % 4, tok // 8
    zi = z % 2
    zmate = z + 1 - 2 * zi
    ztwin = 3 - z
    home = xl == core
    up, down, across = (y + 1) % 4, (y + 3) % 4, (y + 2) % 4
    shard = zi * 4 + y

    def send_row(n):
        slot, (dy, dz, cc) = n // 16, ORDER[n % 16]
        kind, k = slot // 2, slot % 2
        y2 = (y + dy) % 4
        z2 = zmate if dz else z
        zrow = z2 if kind else 3 - z2
        start = ((zrow * 4 + y2) * 2 + cc) * 512 + k * 256
        src = hidden.at[0, :, pl.ds(pl.multiple_of(start, 256), 256)]
        dst = rows.at[slot, shard * 2 + xl]
        where = device(xh, core, y2, z2, cc)
        away = remote(src, dst, rows_s.at[slot], rows_r.at[slot], where)
        if dy == 0 and dz == 0:
            mine = jnp.logical_and(home, core == cc)

            @pl.when(mine)
            def _():
                pltpu.make_async_copy(src, dst, rows_r.at[slot]).start()

            pl.when(jnp.logical_not(mine))(away.start)
        else:
            away.start()

    def send_rows(point):
        for n in range(sum(PACE[:point]), sum(PACE[:point + 1])):
            send_row(n)

    barrier = pltpu.get_barrier_semaphore()
    partners = [(xh, (xl + dl) % 2, (y + dy) % 4, z2, (core + dc) % 2)
                for dl in range(2) for dy in range(4) for z2 in (z, zmate) for dc in range(2)][1:]
    partners += [(1 - xh, dl, y, z, dc) for dl in range(2) for dc in range(2)]
    partners += [(h2, dl, y, ztwin, core) for h2 in (xh, 1 - xh) for dl in range(2)]
    for partner in partners:
        pl.semaphore_signal(barrier, inc=1, device_id=device(*partner), device_id_type=MESH)

    token = tok * 128 + lax.broadcasted_iota(jnp.int32, (128, 256), 0)
    keep = token < lengths[0]
    for q in range(8):
        lane, p = q // 4, q % 4
        start = (((1 - xh if p < 2 else xh) * 2 + lane) * 2 + p % 2) * 256
        part = cotangent[0, :, pl.ds(pl.multiple_of(start, 256), 256)]
        masked[q] = jnp.where(keep, part, jnp.zeros((128, 256), jnp.bfloat16))

    pl.semaphore_wait(barrier, len(partners))

    spot = pl.ds(pl.multiple_of(xl * 128, 128), 128)

    def swap(lane):
        src = masked.at[lane * 4:lane * 4 + 4]
        dst = cols.at[lane * 4:lane * 4 + 4, shard, spot]
        return src, dst

    for lane in (0, 1):
        src, dst = swap(lane)
        mine = jnp.logical_and(home, core == lane)

        @pl.when(mine)
        def _():
            pltpu.make_async_copy(src, dst, swap_r.at[xl]).start()

        @pl.when(jnp.logical_not(mine))
        def _():
            remote(src, dst, swap_s.at[lane], swap_r.at[xl], device(xh, core, y, z, lane)).start()

    send_rows(0)

    for half in (0, 1):
        take(masked.at[0:4], swap_r.at[half])

    def piece(p, which, part=None):
        ref = cols.at[p, which]
        if part is None:
            return ref
        return ref.at[part * 128:part * 128 + 128]

    def pass_on(p, which, sem, where, part=None):
        ref = piece(p, which, part)
        remote(ref, ref, ring_s, ring_r.at[sem], where).start()

    def got(p, sem, part=None):
        take(piece(p, 0, part), ring_r.at[sem])

    mate, own = (1 - zi) * 4, zi * 4

    def lane0(step, p):
        here = lambda y2, z2: device(xh, xl, y2, z2, 0)
        if step == 0:
            pass_on(p, shard, p, here(y, zmate))
            pass_on(p, shard, 4 + p, here(up, z))
            pass_on(p, shard, 12 + p, here(down, z))
        if step == 1:
            got(p, p)
            pass_on(p, mate + y, 8 + p, here(up, z))
            pass_on(p, mate + y, 16 + p, here(down, z))
        if step in (1, 2):
            base, m = (own, 0) if step == 1 else (mate, 1)
            got(p, 4 + m * 4 + p)
            pass_on(p, base + down, 20 + m * 4 + p, here(up, z), 0)
            got(p, 12 + m * 4 + p)
            pass_on(p, base + up, 28 + m * 4 + p, here(down, z), 1)
        if step == 3:
            for m in (0, 1):
                got(p, 20 + m * 4 + p, 0)
                got(p, 28 + m * 4 + p, 1)
            remote(cols.at[p], cols.at[p], side_s.at[p], side_r.at[p], device(xh, xl, y, z, 1)).start()

    def lane1(step, p):
        here = lambda y2, z2: device(xh, xl, y2, z2, 1)
        if step == 0:
            pass_on(4 + p, shard, p, here(up, z))
            pass_on(4 + p, shard, 4 + p, here(down, z))
            pass_on(4 + p, shard, 16 + p, here(y, zmate))
        if step == 1:
            got(4 + p, p)
            pass_on(4 + p, own + down, 8 + p, here(up, z), 0)
            pass_on(4 + p, own + down, 20 + p, here(y, zmate))
            got(4 + p, 4 + p)
            pass_on(4 + p, own + up, 12 + p, here(down, z), 1)
            pass_on(4 + p, own + up, 24 + p, here(y, zmate))
        if step == 2:
            got(4 + p, 8 + p, 0)
            got(4 + p, 12 + p, 1)
            pass_on(4 + p, own + across, 28 + p, here(y, zmate))
        if step == 3:
            for kind in range(4):
                got(4 + p, 16 + kind * 4 + p)
            remote(cols.at[4 + p], cols.at[4 + p], side_s.at[p], side_r.at[p], device(xh, xl, y, z, 0)).start()

    def turn(slot):
        take(rows.at[slot], rows_r.at[slot])
        for s in range(16):
            turned[slot, :, s * 128:(s + 1) * 128] = rows[slot, s].T

    def product(left, q):
        right = cols[q].reshape(2048, 256)
        return lax.dot_general(left, right, (((1,), (0,)), ((), ())), preferred_element_type=jnp.float32)

    twin = device(xh, xl, y, ztwin, core)

    def t_data(q, k):
        return remote(t_code.at[q, k], t_got.at[q, k], ts_s.at[q, k], ts_r.at[q, k], twin)

    def t_scale(q, k):
        return remote(t_step.at[q, k], t_gotstep.at[q, k], tt_s.at[q, k], tt_r.at[q, k], twin)

    def t_part(p, k):
        def one(lane, carry):
            q = lane * 4 + p
            code, step = coded(product(turned[k], q))
            t_code[q, k] = code
            t_step[q, k] = jnp.broadcast_to(step, (8, 256))
            t_data(q, k).start()
            t_scale(q, k).start()
            return carry

        lax.fori_loop(0, 2, one, 0)

    for tick in range(8):
        for lane, steps in enumerate((lane0, lane1)):
            @pl.when(core == lane)
            def _():
                for p in range(4):
                    if 0 <= tick - p <= 3:
                        steps(tick - p, p)
        send_rows(1 + tick)
        if tick == 4:
            turn(0)
        if tick >= 4:
            take(cols.at[0], side_r.at[tick - 4])
            t_part(tick - 4, 0)

    turn(1)
    for p in range(4):
        send_rows(9 + p)
        t_part(p, 1)

    square[...] = jnp.zeros_like(square)
    slot_x = xh * 2 + xl

    def x_parts(k, jj):
        xt, jc = (1 - xh if jj < 2 else xh), jj % 2
        mine = jnp.logical_and(home, jc == core) if jj >= 2 else None
        where = device(xt, core, y, z, jc)
        data = (x_code.at[k, jj], x_got.at[slot_x, k])
        scale = (x_step.at[k, jj], x_gotstep.at[slot_x, k])
        return mine, where, data, scale

    def o_pass(k, carry):
        turn(2 + k)
        for jj in range(4):
            def one(h, inner, jj=jj):
                q = (jj % 2) * 4 + (jj // 2) * 2 + h
                value = product(turned[2 + k], q)
                take(t_got.at[q, k], ts_r.at[q, k])
                take(t_gotstep.at[q, k], tt_r.at[q, k])
                value = value + t_got[q, k].astype(jnp.int32).astype(jnp.float32) * t_gotstep[q, k, 0:1]
                square[...] += jnp.sum((value * value).reshape(32, 8, 256), axis=0)
                code, step = coded(value)
                x_code[k, jj, h] = code
                x_step[k, jj, h] = jnp.broadcast_to(step, (8, 256))
                return inner

            lax.fori_loop(0, 2, one, 0)
            mine, where, data, scale = x_parts(k, jj)

            def away():
                remote(*data, xs_s.at[k, jj], xs_r.at[slot_x, k], where).start()
                remote(*scale, xt_s.at[k, jj], xt_r.at[slot_x, k], where).start()

            def near_by():
                pltpu.make_async_copy(*data, xs_r.at[slot_x, k]).start()
                pltpu.make_async_copy(*scale, xt_r.at[slot_x, k]).start()

            if mine is None:
                away()
            else:
                pl.when(mine)(near_by)
                pl.when(jnp.logical_not(mine))(away)
        return carry

    lax.fori_loop(0, 2, o_pass, 0)

    spot1 = shard * 2 + core
    near[spot1] = square[:, 0:128] + square[:, 128:256]
    for dy, dz, dc in [(2, 1, 1), (2, 1, 0), (2, 0, 1), (2, 0, 0), (1, 1, 1), (3, 1, 1), (1, 1, 0), (3, 1, 0),
                       (1, 0, 1), (3, 0, 1), (1, 0, 0), (3, 0, 0), (0, 1, 1), (0, 1, 0), (0, 0, 1)]:
        remote(near.at[spot1], near.at[spot1], near_s, near_r,
               device(xh, xl, (y + dy) % 4, zmate if dz else z, (core + dc) % 2)).start()
    take(near.at[0:15], near_r)
    spot2 = slot_x * 2 + z // 2
    far[spot2] = jnp.sum(near[...], axis=0)
    for dh, dl, dz in [(1, 0, 1), (1, 1, 1), (1, 0, 0), (1, 1, 0), (0, 1, 1), (0, 0, 1), (0, 1, 0)]:
        remote(far.at[spot2], far.at[spot2], far_s, far_r,
               device((xh + dh) % 2, (xl + dl) % 2, y, ztwin if dz else z, core)).start()
    take(far.at[0:7], far_r)

    factors = []
    for x in range(4):
        total = jnp.sum(far[x * 2] + far[x * 2 + 1], axis=(0, 1), keepdims=True)
        factors.append(jnp.minimum(1.0, clip_bound / jnp.sqrt(total + epsilon)) * scaling)

    for k in range(2):
        for x in range(4):
            take(x_got.at[x, k], xs_r.at[x, k])
            take(x_gotstep.at[x, k], xt_r.at[x, k])
        for h in (0, 1):
            total = None
            for x in range(4):
                weight = factors[x] * x_gotstep[x, k, h, 0:1]
                term = x_got[x, k, h].astype(jnp.int32).astype(jnp.float32) * weight
                total = term if total is None else total + term
            out[k * 256:(k + 1) * 256, h * 256:(h + 1) * 256] = total

    for lane in (0, 1):
        src, dst = swap(lane)

        @pl.when(jnp.logical_not(jnp.logical_and(home, core == lane)))
        def _():
            take(src, swap_s.at[lane])

    take(cols.at[0:7, 0:4], ring_s)
    for p in range(4):
        take(cols.at[0], side_s.at[p])
    for slot in range(4):
        @pl.when(home)
        def _():
            take(rows.at[slot, 0:15], rows_s.at[slot])

        @pl.when(jnp.logical_not(home))
        def _():
            take(rows.at[slot], rows_s.at[slot])
    for k in range(2):
        for q in range(8):
            take(t_code.at[q, k], ts_s.at[q, k])
            take(t_step.at[q, k], tt_s.at[q, k])
        for jj in range(4):
            mine = x_parts(k, jj)[0]

            def gone():
                take(x_code.at[k, jj], xs_s.at[k, jj])
                take(x_step.at[k, jj], xt_s.at[k, jj])

            if mine is None:
                gone()
            else:
                pl.when(jnp.logical_not(mine))(gone)
    take(near.at[0:15], near_s)
    take(far.at[0:7], far_s)


def body(hidden, cotangent, lengths):
    tok_count = lax.axis_size("tok")
    user_count = lax.axis_size("user")
    hidden_width = hidden.shape[2]
    model_width = cotangent.shape[2]
    capacity = hidden.shape[1] * tok_count
    clip_bound = math.sqrt(8.0 * hidden_width * model_width * capacity)
    scaling = math.sqrt(hidden_width * model_width) / (user_count * clip_bound)
    half, full, word = jnp.bfloat16, jnp.float32, jnp.int16
    dma = pltpu.SemaphoreType.DMA
    return pl.pallas_call(
        functools.partial(kernel, clip_bound, scaling),
        out_shape=jax.ShapeDtypeStruct((512, 512), full),
        in_specs=[
            pl.BlockSpec(memory_space=pltpu.SMEM),
            pl.BlockSpec(memory_space=pl.ANY),
            pl.BlockSpec(memory_space=pltpu.VMEM),
        ],
        out_specs=pl.BlockSpec(memory_space=pltpu.VMEM),
        scratch_shapes=[
            pltpu.VMEM((8, 128, 256), half),
            pltpu.VMEM((8, 8, 256, 256), half),
            pltpu.VMEM((4, 16, 128, 256), half),
            pltpu.VMEM((4, 256, 2048), half),
            pltpu.VMEM((8, 2, 256, 256), word),
            pltpu.VMEM((8, 2, 8, 256), full),
            pltpu.VMEM((8, 2, 256, 256), word),
            pltpu.VMEM((8, 2, 8, 256), full),
            pltpu.VMEM((2, 4, 2, 256, 256), word),
            pltpu.VMEM((2, 4, 2, 8, 256), full),
            pltpu.VMEM((4, 2, 2, 256, 256), word),
            pltpu.VMEM((4, 2, 2, 8, 256), full),
            pltpu.VMEM((8, 256), full),
            pltpu.VMEM((16, 8, 128), full),
            pltpu.VMEM((8, 8, 128), full),
            dma((2,)), dma((2,)), dma, dma((36,)), dma((4,)), dma((4,)), dma((4,)), dma((4,)),
            dma((8, 2)), dma((8, 2)), dma((8, 2)), dma((8, 2)),
            dma((2, 4)), dma((4, 2)), dma((2, 4)), dma((4, 2)),
            dma, dma, dma, dma,
        ],
        compiler_params=pltpu.CompilerParams(collective_id=0, has_side_effects=True, vmem_limit_bytes=56 << 20),
        name="clipped_sum",
    )(lengths, hidden, cotangent)


def solution(mesh):
    return jax.shard_map(
        body,
        mesh=mesh,
        in_specs=(P("user", "tok", None), P("user", "tok", None), P("user")),
        out_specs=P("tok", "user"),
        check_vma=False,
    )
```

```python
import functools
import math

import jax
import jax.numpy as jnp
from jax import lax
from jax.experimental import pallas as pl
from jax.experimental.pallas import tpu as pltpu
from jax.sharding import PartitionSpec as P

epsilon = 1e-06
MESH = pl.DeviceIdType.MESH
LEVELS = 32767.0
PARTS = 4
DEEP = 512 // PARTS
ORDER = [(1, 0, 0), (3, 1, 1), (2, 0, 1), (0, 1, 0), (3, 0, 0), (1, 1, 1), (0, 1, 1), (2, 1, 0),
         (1, 0, 1), (3, 1, 0), (2, 0, 0), (3, 0, 1), (2, 1, 1), (1, 1, 0), (0, 0, 0), (0, 0, 1)]
PACE = (48, 0, 0, 0, 0, 0, 16, 32, 16, 16, 0, 0)
SLOTS = [(0, 0), (0, 1), (0, 2), (0, 3), (1, 0), (1, 1), (1, 2), (1, 3)]


def device(xh, xl, y, z, core):
    return (xh * 2 + core, (z * 4 + y) * 2 + xl)


def remote(src, dst, send, recv, where):
    return pltpu.make_async_remote_copy(
        src_ref=src, dst_ref=dst, send_sem=send, recv_sem=recv, device_id=where, device_id_type=MESH
    )


def take(ref, sem):
    pltpu.make_async_copy(ref, ref, sem).wait()


def coded(block):
    peak = jnp.max(jnp.abs(block), axis=0, keepdims=True)
    ok = peak > 1e-30
    step = jnp.where(ok, peak * (1.0 / LEVELS), 0.0)
    inverse = jnp.where(ok, LEVELS / jnp.where(ok, peak, 1.0), 0.0)
    code = jnp.round(block * inverse).astype(jnp.int32).astype(jnp.int16)
    return code, step


def kernel(
    clip_bound, scaling,
    lengths, hidden, cotangent, out,
    drafts, final, masked, cols, rows, turned, t_code, t_step, t_got, t_gotstep,
    x_code, x_step, x_got, x_gotstep, square, near, far,
    draft_r, swap_s, swap_r, ring_s, ring_r, side_s, side_r, rows_s, rows_r,
    ts_s, ts_r, tt_s, tt_r, xs_s, xs_r, xt_s, xt_r, near_s, near_r, far_s, far_r,
):
    user, tok = lax.axis_index("user"), lax.axis_index("tok")
    xh, core = user // 2, user % 2
    xl, y, z = tok % 2, (tok // 2) % 4, tok // 8
    zi = z % 2
    zmate = z + 1 - 2 * zi
    ztwin = 3 - z
    home = xl == core
    up, down, across = (y + 1) % 4, (y + 3) % 4, (y + 2) % 4
    shard = zi * 4 + y

    def send_row(n):
        (kind, k), (dy, dz, cc) = SLOTS[n // 16], ORDER[n % 16]
        slot = kind * PARTS + k
        y2 = (y + dy) % 4
        z2 = zmate if dz else z
        zrow = z2 if kind else 3 - z2
        start = ((zrow * 4 + y2) * 2 + cc) * 512 + k * DEEP
        src = hidden.at[0, :, pl.ds(pl.multiple_of(start, DEEP), DEEP)]
        dst = rows.at[slot, shard * 2 + xl]
        where = device(xh, core, y2, z2, cc)
        away = remote(src, dst, rows_s.at[slot], rows_r.at[slot], where)
        if dy == 0 and dz == 0:
            mine = jnp.logical_and(home, core == cc)

            @pl.when(mine)
            def _():
                pltpu.make_async_copy(src, dst, rows_r.at[slot]).start()

            pl.when(jnp.logical_not(mine))(away.start)
        else:
            away.start()

    def send_rows(point):
        for n in range(sum(PACE[:point]), sum(PACE[:point + 1])):
            send_row(n)

    draft = pltpu.make_async_copy(cotangent.at[0], drafts, draft_r)
    draft.start()
    barrier = pltpu.get_barrier_semaphore()
    partners = [(xh, (xl + dl) % 2, (y + dy) % 4, z2, (core + dc) % 2)
                for dl in range(2) for dy in range(4) for z2 in (z, zmate) for dc in range(2)][1:]
    partners += [(1 - xh, dl, y, z, dc) for dl in range(2) for dc in range(2)]
    partners += [(h2, dl, y, ztwin, core) for h2 in (xh, 1 - xh) for dl in range(2)]
    for partner in partners:
        pl.semaphore_signal(barrier, inc=1, device_id=device(*partner), device_id_type=MESH)

    token = tok * 128 + lax.broadcasted_iota(jnp.int32, (128, 256), 0)
    keep = token < lengths[0]
    draft.wait()
    for q in range(8):
        lane, p = q // 4, q % 4
        start = (((1 - xh if p < 2 else xh) * 2 + lane) * 2 + p % 2) * 256
        part = drafts[:, pl.ds(pl.multiple_of(start, 256), 256)]
        masked[q] = jnp.where(keep, part, jnp.zeros((128, 256), jnp.bfloat16))

    pl.semaphore_wait(barrier, len(partners))

    spot = pl.ds(pl.multiple_of(xl * 128, 128), 128)

    def swap(lane):
        src = masked.at[lane * 4:lane * 4 + 4]
        dst = cols.at[lane * 4:lane * 4 + 4, shard, spot]
        return src, dst

    for lane in (0, 1):
        src, dst = swap(lane)
        mine = jnp.logical_and(home, core == lane)

        @pl.when(mine)
        def _():
            pltpu.make_async_copy(src, dst, swap_r.at[xl]).start()

        @pl.when(jnp.logical_not(mine))
        def _():
            remote(src, dst, swap_s.at[lane], swap_r.at[xl], device(xh, core, y, z, lane)).start()

    send_rows(0)

    for half in (0, 1):
        take(masked.at[0:4], swap_r.at[half])

    def piece(p, which, part=None):
        ref = cols.at[p, which]
        if part is None:
            return ref
        return ref.at[part * 128:part * 128 + 128]

    def pass_on(p, which, sem, where, part=None):
        ref = piece(p, which, part)
        remote(ref, ref, ring_s, ring_r.at[sem], where).start()

    def got(p, sem, part=None):
        take(piece(p, 0, part), ring_r.at[sem])

    mate, own = (1 - zi) * 4, zi * 4

    def lane0(step, p):
        here = lambda y2, z2: device(xh, xl, y2, z2, 0)
        if step == 0:
            pass_on(p, shard, p, here(y, zmate))
            pass_on(p, shard, 4 + p, here(up, z))
            pass_on(p, shard, 12 + p, here(down, z))
        if step == 1:
            got(p, p)
            pass_on(p, mate + y, 8 + p, here(up, z))
            pass_on(p, mate + y, 16 + p, here(down, z))
        if step in (1, 2):
            base, m = (own, 0) if step == 1 else (mate, 1)
            got(p, 4 + m * 4 + p)
            pass_on(p, base + down, 20 + m * 4 + p, here(up, z), 0)
            got(p, 12 + m * 4 + p)
            pass_on(p, base + up, 28 + m * 4 + p, here(down, z), 1)
        if step == 3:
            for m in (0, 1):
                got(p, 20 + m * 4 + p, 0)
                got(p, 28 + m * 4 + p, 1)
            remote(cols.at[p], cols.at[p], side_s.at[p], side_r.at[p], device(xh, xl, y, z, 1)).start()

    def lane1(step, p):
        here = lambda y2, z2: device(xh, xl, y2, z2, 1)
        if step == 0:
            pass_on(4 + p, shard, p, here(up, z))
            pass_on(4 + p, shard, 4 + p, here(down, z))
            pass_on(4 + p, shard, 16 + p, here(y, zmate))
        if step == 1:
            got(4 + p, p)
            pass_on(4 + p, own + down, 8 + p, here(up, z), 0)
            pass_on(4 + p, own + down, 20 + p, here(y, zmate))
            got(4 + p, 4 + p)
            pass_on(4 + p, own + up, 12 + p, here(down, z), 1)
            pass_on(4 + p, own + up, 24 + p, here(y, zmate))
        if step == 2:
            got(4 + p, 8 + p, 0)
            got(4 + p, 12 + p, 1)
            pass_on(4 + p, own + across, 28 + p, here(y, zmate))
        if step == 3:
            for kind in range(4):
                got(4 + p, 16 + kind * 4 + p)
            remote(cols.at[4 + p], cols.at[4 + p], side_s.at[p], side_r.at[p], device(xh, xl, y, z, 0)).start()

    def turn(slot):
        take(rows.at[slot], rows_r.at[slot])
        for s in range(16):
            turned[slot, :, s * 128:(s + 1) * 128] = rows[slot, s].T

    def product(left, q):
        right = cols[q].reshape(2048, 256)
        return lax.dot_general(left, right, (((1,), (0,)), ((), ())), preferred_element_type=jnp.float32)

    twin = device(xh, xl, y, ztwin, core)

    def t_data(q, k):
        return remote(t_code.at[q, k], t_got.at[q, k], ts_s.at[q, k], ts_r.at[q, k], twin)

    def t_scale(q, k):
        return remote(t_step.at[q, k], t_gotstep.at[q, k], tt_s.at[q, k], tt_r.at[q, k], twin)

    def both(slot):
        return turned[slot:slot + 2].reshape(2 * DEEP, 2048)

    def t_two(q, k):
        value = product(both(k), q)
        for i in (0, 1):
            code, step = coded(value[i * DEEP:(i + 1) * DEEP])
            t_code[q, k + i] = code
            t_step[q, k + i] = step
            t_data(q, k + i).start()
            t_scale(q, k + i).start()

    for tick in range(8):
        for lane, steps in enumerate((lane0, lane1)):
            @pl.when(core == lane)
            def _():
                for p in range(4):
                    if 0 <= tick - p <= 3:
                        steps(tick - p, p)
        send_rows(1 + tick)
        if tick == 4:
            turn(0)
            turn(1)
        if tick >= 4:
            take(cols.at[0], side_r.at[tick - 4])


            def one(lane, carry, tick=tick):
                t_two(lane * 4 + tick - 4, 0)
                return carry

            lax.fori_loop(0, 2, one, 0)

    square[...] = jnp.zeros_like(square)
    slot_x = xh * 2 + xl

    def x_parts(k, jj):
        xt, jc = (1 - xh if jj < 2 else xh), jj % 2
        mine = jnp.logical_and(home, jc == core) if jj >= 2 else None
        where = device(xt, core, y, z, jc)
        data = (x_code.at[k, jj], x_got.at[slot_x, k])
        scale = (x_step.at[k, jj], x_gotstep.at[slot_x, k])
        return mine, where, data, scale

    def o_sum(k, q, value):
        take(t_got.at[q, k], ts_r.at[q, k])
        take(t_gotstep.at[q, k], tt_r.at[q, k])
        value = value + t_got[q, k].astype(jnp.int32).astype(jnp.float32) * t_gotstep[q, k]
        square[...] += jnp.sum((value * value).reshape(DEEP // 8, 8, 256), axis=0)
        return value

    def o_at(jj, h):
        return (jj % 2) * 4 + (jj // 2) * 2 + h

    def o_code(k, jj, h, value):
        code, step = coded(value)
        x_code[k, jj, h] = code
        x_step[k, jj, h] = step

    def o_send(k, jj):
        mine, where, data, scale = x_parts(k, jj)

        def away():
            remote(*data, xs_s.at[k, jj], xs_r.at[slot_x, k], where).start()
            remote(*scale, xt_s.at[k, jj], xt_r.at[slot_x, k], where).start()

        def near_by():
            pltpu.make_async_copy(*data, xs_r.at[slot_x, k]).start()
            pltpu.make_async_copy(*scale, xt_r.at[slot_x, k]).start()

        if mine is None:
            away()
        else:
            pl.when(mine)(near_by)
            pl.when(jnp.logical_not(mine))(away)

    send_rows(9)
    turn(2)
    turn(3)

    def late(n, carry):
        t_two((n % 2) * 4 + n // 2, 2)
        return carry

    lax.fori_loop(0, 8, late, 0)
    send_rows(10)

    turn(PARTS)
    turn(PARTS + 1)
    for jj in range(4):
        def one(h, carry, jj=jj):
            q = o_at(jj, h)
            value = product(both(PARTS), q)
            for i in (0, 1):
                o_code(i, jj, h, o_sum(i, q, value[i * DEEP:(i + 1) * DEEP]))
            return carry

        lax.fori_loop(0, 2, one, 0)
        o_send(0, jj)
        o_send(1, jj)
    send_rows(11)

    turn(PARTS + 2)
    for jj in range(4):
        def one(h, carry, jj=jj):
            q = o_at(jj, h)
            o_code(2, jj, h, o_sum(2, q, product(turned[PARTS + 2], q)))
            return carry

        lax.fori_loop(0, 2, one, 0)
        o_send(2, jj)

    last = PARTS - 1
    turn(PARTS + last)

    def draft_of(n, carry):
        jj, h = n // 2, n % 2
        q = o_at(jj, h)
        final[n] = o_sum(last, q, product(turned[PARTS + last], q))
        return carry

    lax.fori_loop(0, 8, draft_of, 0)

    spot1 = shard * 2 + core
    near[spot1] = square[:, 0:128] + square[:, 128:256]
    for dy, dz, dc in [(2, 1, 1), (2, 1, 0), (2, 0, 1), (2, 0, 0), (1, 1, 1), (3, 1, 1), (1, 1, 0), (3, 1, 0),
                       (1, 0, 1), (3, 0, 1), (1, 0, 0), (3, 0, 0), (0, 1, 1), (0, 1, 0), (0, 0, 1)]:
        remote(near.at[spot1], near.at[spot1], near_s, near_r,
               device(xh, xl, (y + dy) % 4, zmate if dz else z, (core + dc) % 2)).start()
    for jj in range(4):
        def one(h, carry, jj=jj):
            o_code(last, jj, h, final[jj * 2 + h])
            return carry

        lax.fori_loop(0, 2, one, 0)
        o_send(last, jj)

    take(near.at[0:15], near_r)
    spot2 = slot_x * 2 + z // 2
    far[spot2] = jnp.sum(near[...], axis=0)
    for dh, dl, dz in [(1, 0, 1), (1, 1, 1), (1, 0, 0), (1, 1, 0), (0, 1, 1), (0, 0, 1), (0, 1, 0)]:
        remote(far.at[spot2], far.at[spot2], far_s, far_r,
               device((xh + dh) % 2, (xl + dl) % 2, y, ztwin if dz else z, core)).start()
    take(far.at[0:7], far_r)

    factors = []
    for x in range(4):
        total = jnp.sum(far[x * 2] + far[x * 2 + 1], axis=(0, 1), keepdims=True)
        factors.append(jnp.minimum(1.0, clip_bound / jnp.sqrt(total + epsilon)) * scaling)

    for k in range(PARTS):
        for x in range(4):
            take(x_got.at[x, k], xs_r.at[x, k])
            take(x_gotstep.at[x, k], xt_r.at[x, k])
        for h in (0, 1):
            total = None
            for x in range(4):
                weight = factors[x] * x_gotstep[x, k, h]
                term = x_got[x, k, h].astype(jnp.int32).astype(jnp.float32) * weight
                total = term if total is None else total + term
            out[k * DEEP:(k + 1) * DEEP, h * 256:(h + 1) * 256] = total

    for lane in (0, 1):
        src, dst = swap(lane)

        @pl.when(jnp.logical_not(jnp.logical_and(home, core == lane)))
        def _():
            take(src, swap_s.at[lane])

    take(cols.at[0:7, 0:4], ring_s)
    for p in range(4):
        take(cols.at[0], side_s.at[p])
    for slot in range(2 * PARTS):
        @pl.when(home)
        def _():
            take(rows.at[slot, 0:15], rows_s.at[slot])

        @pl.when(jnp.logical_not(home))
        def _():
            take(rows.at[slot], rows_s.at[slot])
    for k in range(PARTS):
        for q in range(8):
            take(t_code.at[q, k], ts_s.at[q, k])
            take(t_step.at[q, k], tt_s.at[q, k])
        for jj in range(4):
            mine = x_parts(k, jj)[0]

            def gone():
                take(x_code.at[k, jj], xs_s.at[k, jj])
                take(x_step.at[k, jj], xt_s.at[k, jj])

            if mine is None:
                gone()
            else:
                pl.when(jnp.logical_not(mine))(gone)
    take(near.at[0:15], near_s)
    take(far.at[0:7], far_s)


def body(hidden, cotangent, lengths):
    tok_count = lax.axis_size("tok")
    user_count = lax.axis_size("user")
    hidden_width = hidden.shape[2]
    model_width = cotangent.shape[2]
    capacity = hidden.shape[1] * tok_count
    clip_bound = math.sqrt(8.0 * hidden_width * model_width * capacity)
    scaling = math.sqrt(hidden_width * model_width) / (user_count * clip_bound)
    half, full, word = jnp.bfloat16, jnp.float32, jnp.int16
    dma = pltpu.SemaphoreType.DMA
    return pl.pallas_call(
        functools.partial(kernel, clip_bound, scaling),
        out_shape=jax.ShapeDtypeStruct((512, 512), full),
        in_specs=[
            pl.BlockSpec(memory_space=pltpu.SMEM),
            pl.BlockSpec(memory_space=pl.ANY),
            pl.BlockSpec(memory_space=pl.ANY),
        ],
        out_specs=pl.BlockSpec(memory_space=pltpu.VMEM),
        scratch_shapes=[
            pltpu.VMEM((128, 2048), half),
            pltpu.VMEM((8, DEEP, 256), full),
            pltpu.VMEM((8, 128, 256), half),
            pltpu.VMEM((8, 8, 256, 256), half),
            pltpu.VMEM((2 * PARTS, 16, 128, DEEP), half),
            pltpu.VMEM((2 * PARTS, DEEP, 2048), half),
            pltpu.VMEM((8, PARTS, DEEP, 256), word),
            pltpu.VMEM((8, PARTS, 1, 256), full),
            pltpu.VMEM((8, PARTS, DEEP, 256), word),
            pltpu.VMEM((8, PARTS, 1, 256), full),
            pltpu.VMEM((PARTS, 4, 2, DEEP, 256), word),
            pltpu.VMEM((PARTS, 4, 2, 1, 256), full),
            pltpu.VMEM((4, PARTS, 2, DEEP, 256), word),
            pltpu.VMEM((4, PARTS, 2, 1, 256), full),
            pltpu.VMEM((8, 256), full),
            pltpu.VMEM((16, 8, 128), full),
            pltpu.VMEM((8, 8, 128), full),
            dma, dma((2,)), dma((2,)), dma, dma((36,)), dma((4,)), dma((4,)), dma((2 * PARTS,)), dma((2 * PARTS,)),
            dma((8, PARTS)), dma((8, PARTS)), dma((8, PARTS)), dma((8, PARTS)),
            dma((PARTS, 4)), dma((4, PARTS)), dma((PARTS, 4)), dma((4, PARTS)),
            dma, dma, dma, dma,
        ],
        compiler_params=pltpu.CompilerParams(collective_id=0, has_side_effects=True, vmem_limit_bytes=56 << 20),
        name="clipped_sum",
    )(lengths, hidden, cotangent)


def solution(mesh):
    return jax.shard_map(
        body,
        mesh=mesh,
        in_specs=(P("user", "tok", None), P("user", "tok", None), P("user")),
        out_specs=P("tok", "user"),
        check_vma=False,
    )
```

```python
import functools
import math

import jax
import jax.numpy as jnp
from jax import lax
from jax.experimental import pallas as pl
from jax.experimental.pallas import tpu as pltpu
from jax.sharding import PartitionSpec as P

epsilon = 1e-06
MESH = pl.DeviceIdType.MESH
LEVELS = 32767.0
PARTS = 4
DEEP = 512 // PARTS
ORDER = [(1, 0, 0), (3, 1, 1), (2, 0, 1), (0, 1, 0), (3, 0, 0), (1, 1, 1), (0, 1, 1), (2, 1, 0),
         (1, 0, 1), (3, 1, 0), (2, 0, 0), (3, 0, 1), (2, 1, 1), (1, 1, 0), (0, 0, 0), (0, 0, 1)]
PACE = (48, 0, 0, 0, 0, 0, 16, 32, 16, 16, 0, 0)
SLOTS = [(0, 0), (0, 1), (0, 2), (0, 3), (1, 0), (1, 1), (1, 2), (1, 3)]


def device(xh, xl, y, z, core):
    return (xh * 2 + core, (z * 4 + y) * 2 + xl)


def remote(src, dst, send, recv, where):
    return pltpu.make_async_remote_copy(
        src_ref=src, dst_ref=dst, send_sem=send, recv_sem=recv, device_id=where, device_id_type=MESH
    )


def take(ref, sem):
    pltpu.make_async_copy(ref, ref, sem).wait()


def coded(block):
    peak = jnp.max(jnp.abs(block), axis=0, keepdims=True)
    ok = peak > 1e-30
    step = jnp.where(ok, peak * (1.0 / LEVELS), 0.0)
    inverse = jnp.where(ok, LEVELS / jnp.where(ok, peak, 1.0), 0.0)
    code = jnp.round(block * inverse).astype(jnp.int32).astype(jnp.int16)
    return code, step


def kernel(
    clip_bound, scaling,
    lengths, hidden, cotangent, out,
    drafts, final, masked, cols, rows, turned, t_code, t_step, t_got, t_gotstep,
    x_code, x_step, x_got, x_gotstep, square, near, far,
    draft_r, swap_s, swap_r, ring_s, ring_r, side_s, side_r, rows_s, rows_r,
    ts_s, ts_r, tt_s, tt_r, xs_s, xs_r, xt_s, xt_r, near_s, near_r, far_s, far_r,
):
    user, tok = lax.axis_index("user"), lax.axis_index("tok")
    xh, core = user // 2, user % 2
    xl, y, z = tok % 2, (tok // 2) % 4, tok // 8
    zi = z % 2
    zmate = z + 1 - 2 * zi
    ztwin = 3 - z
    home = xl == core
    up, down, across = (y + 1) % 4, (y + 3) % 4, (y + 2) % 4
    shard = zi * 4 + y

    def send_row(n):
        (kind, k), (dy, dz, cc) = SLOTS[n // 16], ORDER[n % 16]
        slot = kind * PARTS + k
        y2 = (y + dy * (1 + 2 * core)) % 4
        z2 = zmate if dz else z
        zrow = z2 if kind else 3 - z2
        start = ((zrow * 4 + y2) * 2 + cc) * 512 + k * DEEP
        src = hidden.at[0, :, pl.ds(pl.multiple_of(start, DEEP), DEEP)]
        dst = rows.at[slot, shard * 2 + xl]
        where = device(xh, core, y2, z2, cc)
        away = remote(src, dst, rows_s.at[slot], rows_r.at[slot], where)
        if dy == 0 and dz == 0:
            mine = jnp.logical_and(home, core == cc)

            @pl.when(mine)
            def _():
                pltpu.make_async_copy(src, dst, rows_r.at[slot]).start()

            pl.when(jnp.logical_not(mine))(away.start)
        else:
            away.start()

    def send_rows(point):
        for n in range(sum(PACE[:point]), sum(PACE[:point + 1])):
            send_row(n)

    draft = pltpu.make_async_copy(cotangent.at[0], drafts, draft_r)
    draft.start()
    barrier = pltpu.get_barrier_semaphore()
    partners = [(xh, (xl + dl) % 2, (y + dy) % 4, z2, (core + dc) % 2)
                for dl in range(2) for dy in range(4) for z2 in (z, zmate) for dc in range(2)][1:]
    partners += [(1 - xh, dl, y, z, dc) for dl in range(2) for dc in range(2)]
    partners += [(h2, dl, y, ztwin, core) for h2 in (xh, 1 - xh) for dl in range(2)]
    for partner in partners:
        pl.semaphore_signal(barrier, inc=1, device_id=device(*partner), device_id_type=MESH)

    token = tok * 128 + lax.broadcasted_iota(jnp.int32, (128, 256), 0)
    keep = token < lengths[0]
    draft.wait()
    for q in range(8):
        lane, p = q // 4, q % 4
        start = (((1 - xh if p < 2 else xh) * 2 + lane) * 2 + p % 2) * 256
        part = drafts[:, pl.ds(pl.multiple_of(start, 256), 256)]
        masked[q] = jnp.where(keep, part, jnp.zeros((128, 256), jnp.bfloat16))

    pl.semaphore_wait(barrier, len(partners))

    spot = pl.ds(pl.multiple_of(xl * 128, 128), 128)

    def swap(lane):
        src = masked.at[lane * 4:lane * 4 + 4]
        dst = cols.at[lane * 4:lane * 4 + 4, shard, spot]
        return src, dst

    for lane in (0, 1):
        src, dst = swap(lane)
        mine = jnp.logical_and(home, core == lane)

        @pl.when(mine)
        def _():
            pltpu.make_async_copy(src, dst, swap_r.at[xl]).start()

        @pl.when(jnp.logical_not(mine))
        def _():
            remote(src, dst, swap_s.at[lane], swap_r.at[xl], device(xh, core, y, z, lane)).start()

    send_rows(0)

    for half in (0, 1):
        take(masked.at[0:4], swap_r.at[half])

    def piece(p, which, part=None):
        ref = cols.at[p, which]
        if part is None:
            return ref
        return ref.at[part * 128:part * 128 + 128]

    def pass_on(p, which, sem, where, part=None):
        ref = piece(p, which, part)
        remote(ref, ref, ring_s, ring_r.at[sem], where).start()

    def got(p, sem, part=None):
        take(piece(p, 0, part), ring_r.at[sem])

    mate, own = (1 - zi) * 4, zi * 4

    def lane0(step, p):
        here = lambda y2, z2: device(xh, xl, y2, z2, 0)
        if step == 0:
            pass_on(p, shard, p, here(y, zmate))
            pass_on(p, shard, 4 + p, here(up, z))
            pass_on(p, shard, 12 + p, here(down, z))
        if step == 1:
            got(p, p)
            pass_on(p, mate + y, 8 + p, here(up, z))
            pass_on(p, mate + y, 16 + p, here(down, z))
        if step in (1, 2):
            base, m = (own, 0) if step == 1 else (mate, 1)
            got(p, 4 + m * 4 + p)
            pass_on(p, base + down, 20 + m * 4 + p, here(up, z), 0)
            got(p, 12 + m * 4 + p)
            pass_on(p, base + up, 28 + m * 4 + p, here(down, z), 1)
        if step == 3:
            for m in (0, 1):
                got(p, 20 + m * 4 + p, 0)
                got(p, 28 + m * 4 + p, 1)
            remote(cols.at[p], cols.at[p], side_s.at[p], side_r.at[p], device(xh, xl, y, z, 1)).start()

    def lane1(step, p):
        here = lambda y2, z2: device(xh, xl, y2, z2, 1)
        if step == 0:
            pass_on(4 + p, shard, p, here(up, z))
            pass_on(4 + p, shard, 4 + p, here(down, z))
            pass_on(4 + p, shard, 16 + p, here(y, zmate))
        if step == 1:
            got(4 + p, p)
            pass_on(4 + p, own + down, 8 + p, here(up, z), 0)
            pass_on(4 + p, own + down, 20 + p, here(y, zmate))
            got(4 + p, 4 + p)
            pass_on(4 + p, own + up, 12 + p, here(down, z), 1)
            pass_on(4 + p, own + up, 24 + p, here(y, zmate))
        if step == 2:
            got(4 + p, 8 + p, 0)
            got(4 + p, 12 + p, 1)
            pass_on(4 + p, own + across, 28 + p, here(y, zmate))
        if step == 3:
            for kind in range(4):
                got(4 + p, 16 + kind * 4 + p)
            remote(cols.at[4 + p], cols.at[4 + p], side_s.at[p], side_r.at[p], device(xh, xl, y, z, 0)).start()

    def turn(slot):
        take(rows.at[slot], rows_r.at[slot])
        for s in range(16):
            turned[slot, :, s * 128:(s + 1) * 128] = rows[slot, s].T

    def product(left, q):
        right = cols[q].reshape(2048, 256)
        return lax.dot_general(left, right, (((1,), (0,)), ((), ())), preferred_element_type=jnp.float32)

    twin = device(xh, xl, y, ztwin, core)

    def t_data(q, k):
        return remote(t_code.at[q, k], t_got.at[q, k], ts_s.at[q, k], ts_r.at[q, k], twin)

    def t_scale(q, k):
        return remote(t_step.at[q, k], t_gotstep.at[q, k], tt_s.at[q, k], tt_r.at[q, k], twin)

    def both(slot):
        return turned[slot:slot + 2].reshape(2 * DEEP, 2048)

    def t_two(q, k):
        value = product(both(k), q)
        for i in (0, 1):
            code, step = coded(value[i * DEEP:(i + 1) * DEEP])
            t_code[q, k + i] = code
            t_step[q, k + i] = step
            t_data(q, k + i).start()
            t_scale(q, k + i).start()

    for tick in range(8):
        for lane, steps in enumerate((lane0, lane1)):
            @pl.when(core == lane)
            def _():
                for p in range(4):
                    if 0 <= tick - p <= 3:
                        steps(tick - p, p)
        send_rows(1 + tick)
        if tick == 4:
            turn(0)
            turn(1)
        if tick >= 4:
            take(cols.at[0], side_r.at[tick - 4])


            def one(lane, carry, tick=tick):
                t_two(lane * 4 + tick - 4, 0)
                return carry

            lax.fori_loop(0, 2, one, 0)

    square[...] = jnp.zeros_like(square)
    slot_x = xh * 2 + xl

    def x_parts(k, jj):
        xt, jc = (1 - xh if jj < 2 else xh), jj % 2
        mine = jnp.logical_and(home, jc == core) if jj >= 2 else None
        where = device(xt, core, y, z, jc)
        data = (x_code.at[k, jj], x_got.at[slot_x, k])
        scale = (x_step.at[k, jj], x_gotstep.at[slot_x, k])
        return mine, where, data, scale

    def o_sum(k, q, value):
        take(t_got.at[q, k], ts_r.at[q, k])
        take(t_gotstep.at[q, k], tt_r.at[q, k])
        value = value + t_got[q, k].astype(jnp.int32).astype(jnp.float32) * t_gotstep[q, k]
        square[...] += jnp.sum((value * value).reshape(DEEP // 8, 8, 256), axis=0)
        return value

    def o_at(jj, h):
        return (jj % 2) * 4 + (jj // 2) * 2 + h

    def o_code(k, jj, h, value):
        code, step = coded(value)
        x_code[k, jj, h] = code
        x_step[k, jj, h] = step

    def o_send(k, jj):
        mine, where, data, scale = x_parts(k, jj)

        def away():
            remote(*data, xs_s.at[k, jj], xs_r.at[slot_x, k], where).start()
            remote(*scale, xt_s.at[k, jj], xt_r.at[slot_x, k], where).start()

        def near_by():
            pltpu.make_async_copy(*data, xs_r.at[slot_x, k]).start()
            pltpu.make_async_copy(*scale, xt_r.at[slot_x, k]).start()

        if mine is None:
            away()
        else:
            pl.when(mine)(near_by)
            pl.when(jnp.logical_not(mine))(away)

    send_rows(9)
    turn(2)
    turn(3)

    def late(n, carry):
        t_two((n % 2) * 4 + n // 2, 2)
        return carry

    lax.fori_loop(0, 8, late, 0)
    send_rows(10)

    turn(PARTS)
    turn(PARTS + 1)
    for jj in range(4):
        def one(h, carry, jj=jj):
            q = o_at(jj, h)
            value = product(both(PARTS), q)
            for i in (0, 1):
                o_code(i, jj, h, o_sum(i, q, value[i * DEEP:(i + 1) * DEEP]))
            return carry

        lax.fori_loop(0, 2, one, 0)
        o_send(0, jj)
        o_send(1, jj)
    send_rows(11)

    turn(PARTS + 2)
    for jj in range(4):
        def one(h, carry, jj=jj):
            q = o_at(jj, h)
            o_code(2, jj, h, o_sum(2, q, product(turned[PARTS + 2], q)))
            return carry

        lax.fori_loop(0, 2, one, 0)
        o_send(2, jj)

    last = PARTS - 1
    turn(PARTS + last)

    def draft_of(n, carry):
        jj, h = n // 2, n % 2
        q = o_at(jj, h)
        final[n] = o_sum(last, q, product(turned[PARTS + last], q))
        return carry

    lax.fori_loop(0, 8, draft_of, 0)

    spot1 = shard * 2 + core
    near[spot1] = square[:, 0:128] + square[:, 128:256]
    for dy, dz, dc in [(2, 1, 1), (2, 1, 0), (2, 0, 1), (2, 0, 0), (1, 1, 1), (3, 1, 1), (1, 1, 0), (3, 1, 0),
                       (1, 0, 1), (3, 0, 1), (1, 0, 0), (3, 0, 0), (0, 1, 1), (0, 1, 0), (0, 0, 1)]:
        remote(near.at[spot1], near.at[spot1], near_s, near_r,
               device(xh, xl, (y + dy) % 4, zmate if dz else z, (core + dc) % 2)).start()
    for jj in range(4):
        def one(h, carry, jj=jj):
            o_code(last, jj, h, final[jj * 2 + h])
            return carry

        lax.fori_loop(0, 2, one, 0)
        o_send(last, jj)

    take(near.at[0:15], near_r)
    spot2 = slot_x * 2 + z // 2
    far[spot2] = jnp.sum(near[...], axis=0)
    for dh, dl, dz in [(1, 0, 1), (1, 1, 1), (1, 0, 0), (1, 1, 0), (0, 1, 1), (0, 0, 1), (0, 1, 0)]:
        remote(far.at[spot2], far.at[spot2], far_s, far_r,
               device((xh + dh) % 2, (xl + dl) % 2, y, ztwin if dz else z, core)).start()
    take(far.at[0:7], far_r)

    factors = []
    for x in range(4):
        total = jnp.sum(far[x * 2] + far[x * 2 + 1], axis=(0, 1), keepdims=True)
        factors.append(jnp.minimum(1.0, clip_bound / jnp.sqrt(total + epsilon)) * scaling)

    for k in range(PARTS):
        for x in range(4):
            take(x_got.at[x, k], xs_r.at[x, k])
            take(x_gotstep.at[x, k], xt_r.at[x, k])
        for h in (0, 1):
            total = None
            for x in range(4):
                weight = factors[x] * x_gotstep[x, k, h]
                term = x_got[x, k, h].astype(jnp.int32).astype(jnp.float32) * weight
                total = term if total is None else total + term
            out[k * DEEP:(k + 1) * DEEP, h * 256:(h + 1) * 256] = total

    for lane in (0, 1):
        src, dst = swap(lane)

        @pl.when(jnp.logical_not(jnp.logical_and(home, core == lane)))
        def _():
            take(src, swap_s.at[lane])

    take(cols.at[0:7, 0:4], ring_s)
    for p in range(4):
        take(cols.at[0], side_s.at[p])
    for slot in range(2 * PARTS):
        @pl.when(home)
        def _():
            take(rows.at[slot, 0:15], rows_s.at[slot])

        @pl.when(jnp.logical_not(home))
        def _():
            take(rows.at[slot], rows_s.at[slot])
    for k in range(PARTS):
        for q in range(8):
            take(t_code.at[q, k], ts_s.at[q, k])
            take(t_step.at[q, k], tt_s.at[q, k])
        for jj in range(4):
            mine = x_parts(k, jj)[0]

            def gone():
                take(x_code.at[k, jj], xs_s.at[k, jj])
                take(x_step.at[k, jj], xt_s.at[k, jj])

            if mine is None:
                gone()
            else:
                pl.when(jnp.logical_not(mine))(gone)
    take(near.at[0:15], near_s)
    take(far.at[0:7], far_s)


def body(hidden, cotangent, lengths):
    tok_count = lax.axis_size("tok")
    user_count = lax.axis_size("user")
    hidden_width = hidden.shape[2]
    model_width = cotangent.shape[2]
    capacity = hidden.shape[1] * tok_count
    clip_bound = math.sqrt(8.0 * hidden_width * model_width * capacity)
    scaling = math.sqrt(hidden_width * model_width) / (user_count * clip_bound)
    half, full, word = jnp.bfloat16, jnp.float32, jnp.int16
    dma = pltpu.SemaphoreType.DMA
    return pl.pallas_call(
        functools.partial(kernel, clip_bound, scaling),
        out_shape=jax.ShapeDtypeStruct((512, 512), full),
        in_specs=[
            pl.BlockSpec(memory_space=pltpu.SMEM),
            pl.BlockSpec(memory_space=pl.ANY),
            pl.BlockSpec(memory_space=pl.ANY),
        ],
        out_specs=pl.BlockSpec(memory_space=pltpu.VMEM),
        scratch_shapes=[
            pltpu.VMEM((128, 2048), half),
            pltpu.VMEM((8, DEEP, 256), full),
            pltpu.VMEM((8, 128, 256), half),
            pltpu.VMEM((8, 8, 256, 256), half),
            pltpu.VMEM((2 * PARTS, 16, 128, DEEP), half),
            pltpu.VMEM((2 * PARTS, DEEP, 2048), half),
            pltpu.VMEM((8, PARTS, DEEP, 256), word),
            pltpu.VMEM((8, PARTS, 1, 256), full),
            pltpu.VMEM((8, PARTS, DEEP, 256), word),
            pltpu.VMEM((8, PARTS, 1, 256), full),
            pltpu.VMEM((PARTS, 4, 2, DEEP, 256), word),
            pltpu.VMEM((PARTS, 4, 2, 1, 256), full),
            pltpu.VMEM((4, PARTS, 2, DEEP, 256), word),
            pltpu.VMEM((4, PARTS, 2, 1, 256), full),
            pltpu.VMEM((8, 256), full),
            pltpu.VMEM((16, 8, 128), full),
            pltpu.VMEM((8, 8, 128), full),
            dma, dma((2,)), dma((2,)), dma, dma((36,)), dma((4,)), dma((4,)), dma((2 * PARTS,)), dma((2 * PARTS,)),
            dma((8, PARTS)), dma((8, PARTS)), dma((8, PARTS)), dma((8, PARTS)),
            dma((PARTS, 4)), dma((4, PARTS)), dma((PARTS, 4)), dma((4, PARTS)),
            dma, dma, dma, dma,
        ],
        compiler_params=pltpu.CompilerParams(collective_id=0, has_side_effects=True, vmem_limit_bytes=56 << 20),
        name="clipped_sum",
    )(lengths, hidden, cotangent)


def solution(mesh):
    return jax.shard_map(
        body,
        mesh=mesh,
        in_specs=(P("user", "tok", None), P("user", "tok", None), P("user")),
        out_specs=P("tok", "user"),
        check_vma=False,
    )
```
